128 devices in a mesh: mem: 8 (over z, y_lo), lev: 16 (over y_hi, x, core).
Axes of the slice: x: 4, y: 4 (y_hi: 2, y_lo: 2; y = y_hi * 2 + y_lo), z: 4, core: 2. Of those that a mesh axis runs over, the one named last changes fastest.
Arguments:
- control: float32 [8, 64, 200, 400], P('mem', 'lev'), may hold values from -6 to 6
- perturbations: bfloat16 [8, 2, 2, 64, 80000], P('mem', None, None, None, 'lev'), may hold values from -4 to 4
- member_scales: float32 [8], P('mem'), may hold values from 0.05 to 0.2
- vertical_loc: float32 [64, 64], replicated, may hold values from -0.75 to 0.75
- latitude_loc: float32 [200, 200], replicated, may hold values from -0.4375 to 0.4375
- longitude_loc: float32 [400, 400], replicated, may hold values from -0.3125 to 0.3125
- observed_index: int32 [2, 65536], P(None, 'lev'), may hold values from 0 to 639999
- observed_weight: float32 [2, 65536], P(None, 'lev'), may hold values from 0.5 to 8
Outputs:
- hessian_vector: float32 [8, 64, 200, 400], P('mem', 'lev')
The draws below stay inside these ranges and needn't reach their ends.
All inputs are finite; a program needn't handle non-finite values.
Results may differ from the reference program's by a relative error of at most 0.0003.
Values sent between devices are 32-bit elements; how exact they have to be, the bound alone decides.
No kernel may reach another device: no remote copies, remote signals or barrier semaphores. Data moves between devices by JAX's collectives and lax.ppermute only.
A program may use at most 192 MiB of HBM per device.

```python
import math
import jax
import jax.numpy as jnp
from jax import lax

LEVELS = 64
LAT = 200
LON = 400
SLOTS = 2
VARS = 2
OBS_DEV = 4096
CELLS = 80000
MEMBERS = 8
OBS = 65536
N_LEV = 16


def with_ends(result, own_key, low, largest):
    extent = result.shape
    spot = [jax.random.randint(jax.random.fold_in(own_key, axis), (), 0, extent[axis]) for axis in range(len(extent))]
    result = result.at[tuple(spot)].set(low)
    longest = extent.index(max(extent))
    spot[longest] = (spot[longest] + 1) % extent[longest]
    return result.at[tuple(spot)].set(largest)


def steps_of(rng, extent, split, smallest, top_value):
    def one(axis_at, shards_of):
        steps = jax.random.uniform(jax.random.fold_in(jax.random.fold_in(rng, 6), axis_at), (shards_of,), jnp.float32, smallest / len(split), top_value / len(split))
        return jnp.repeat(jnp.exp(steps), extent[axis_at] // shards_of).reshape((-1,) + (1,) * (len(extent) - axis_at - 1))

    gain = one(*split[0])
    for cut in split[1:]:
        gain = gain * one(*cut)
    return gain


def bell_draw(rng, extent, deviation, bound, pieces=(), kind=jnp.bfloat16):
    factor_of = steps_of(rng, extent, pieces, -0.22, 0.18) if pieces else 1.0
    drawn = jax.random.normal(rng, extent, jnp.float32) * deviation * factor_of
    return jnp.minimum(jnp.maximum(drawn, -bound), bound).astype(kind)


def setup_inputs(seed: int = 0) -> dict:
    splits = jax.random.split(jax.random.key(seed), 9)
    return {
        "control": bell_draw(splits[0], (MEMBERS, LEVELS, LAT, LON), 1.0, 6.0, ((0, 8), (1, 16)), jnp.float32),
        "perturbations": bell_draw(splits[1], (MEMBERS, SLOTS, VARS, LEVELS, CELLS), 1.0, 4.0, ((0, 8), (4, 16))),
        "member_scales": jnp.clip(jnp.exp(math.log(0.2) - 1.3862944 * jax.random.uniform(splits[2], (MEMBERS,), jnp.float32) ** steps_of(splits[2], (MEMBERS,), ((0, 8),), -0.2, 0.2)), 0.05, 0.2),
        "vertical_loc": bell_draw(splits[3], (LEVELS, LEVELS), LEVELS ** -0.5, 0.75, (), jnp.float32),
        "latitude_loc": bell_draw(splits[4], (LAT, LAT), LAT ** -0.5, 0.4375, (), jnp.float32),
        "longitude_loc": bell_draw(splits[5], (LON, LON), LON ** -0.5, 0.3125, (), jnp.float32),
        "observed_index": with_ends(jax.random.randint(splits[6], (SLOTS, OBS), 0, VARS * LEVELS * (CELLS // N_LEV)), jax.random.fold_in(splits[6], 1), 0, (VARS * LEVELS * (CELLS // N_LEV)) - 1).astype(jnp.int32),
        "observed_weight": jnp.clip(jnp.exp(math.log(8.0) - 2.7725887 * jax.random.uniform(splits[7], (SLOTS, OBS), jnp.float32) ** steps_of(splits[7], (SLOTS, OBS), ((1, 16),), -0.2, 0.2)), 0.5, 8.0),
    }


HIGH = lax.Precision.HIGHEST


def reference(control, perturbations, member_scales, vertical_loc, latitude_loc, longitude_loc, observed_index, observed_weight):
    def forward(carry, item):
        field, member_pert, scale = item
        rows = jnp.einsum('ab,lbq->laq', latitude_loc, field, precision=HIGH)
        horizontal = jnp.einsum('laq,oq->lao', rows, longitude_loc, precision=HIGH).reshape(LEVELS, CELLS)
        localized = jnp.einsum('lk,kp->lp', vertical_loc, horizontal, precision=HIGH)
        return carry + scale * (member_pert.astype(jnp.float32) * localized[None, None]), None

    start = jnp.zeros((SLOTS, VARS, LEVELS, CELLS), jnp.float32)
    increment, _ = lax.scan(forward, start, (control, perturbations, member_scales))
    column_width = CELLS // N_LEV
    block = (jnp.arange(OBS, dtype=jnp.int32) // OBS_DEV).astype(jnp.int32)
    variable = observed_index // (LEVELS * column_width)
    level = (observed_index // column_width) % LEVELS
    cell = block[None, :] * column_width + observed_index % column_width
    flat_index = ((variable * LEVELS + level) * CELLS + cell).astype(jnp.int32)
    slot_rows = jnp.arange(SLOTS, dtype=jnp.int32)[:, None]
    obs_grid = jnp.zeros((SLOTS, VARS * LEVELS * CELLS), jnp.float32).at[slot_rows, flat_index].add(observed_weight)
    innovation_adj = obs_grid.reshape(SLOTS, VARS, LEVELS, CELLS) * increment

    def adjoint(item):
        field, member_pert, scale = item
        member_adj = scale * jnp.sum(member_pert.astype(jnp.float32) * innovation_adj, axis=(0, 1))
        vertical_adj = jnp.einsum('kl,kp->lp', vertical_loc, member_adj, precision=HIGH).reshape(LEVELS, LAT, LON)
        rows = jnp.einsum('ba,lbq->laq', latitude_loc, vertical_adj, precision=HIGH)
        return field + jnp.einsum('laq,qo->lao', rows, longitude_loc, precision=HIGH)

    return lax.map(adjoint, (control, perturbations, member_scales))
```

```python
import functools

import jax
import jax.numpy as jnp
from jax import lax
from jax.experimental import pallas as pl
from jax.experimental.pallas import tpu as pltpu
from jax.sharding import PartitionSpec as P

F32 = jnp.float32
BF16 = jnp.bfloat16
I32 = jnp.int32

NB = 32
OB = 256
NK = 20
YS = 136
NN = (((1,), (0,)), ((), ()))
NT = (((1,), (1,)), ((), ()))
TN = (((0,), (0,)), ((), ()))


def split(x):
    hi = x.astype(BF16)
    return hi, (x - hi.astype(F32)).astype(BF16)


def mm(a, b, dims):
    return lax.dot_general(a, b, dims, preferred_element_type=F32)


def mm3(a, b, dims=NN):
    return mm(a[0], b[0], dims) + (mm(a[0], b[1], dims) + mm(a[1], b[0], dims))


def pad_latitude(a_ref, ap_ref):
    ap_ref[...] = jnp.zeros_like(ap_ref)
    for i in range(8):
        row = (i % 2) * 128 + (i // 2) * 32
        ap_ref[row : row + 25, :] = a_ref[25 * i : 25 * i + 25, :]


def iota(shape, dim):
    return lax.broadcasted_iota(I32, shape, dim)


def forward_kernel(c_ref, a_ref, o_ref, f_ref, ap_ref, y_ref):
    pad_latitude(a_ref, ap_ref)
    lat = split(ap_ref[...])
    lon = split(o_ref[...])
    for l in range(4):
        rows = mm3(split(c_ref[l]), lon, NT)
        field = mm3(lat, split(rows))
        for u in range(2):
            base = (4 * u + l) * YS
            part = field[128 * u : 128 * u + 128]
            for j in range(3):
                y_ref[j, base : base + 128, :] = part[:, 128 * j : 128 * j + 128]
            y_ref[3, base : base + 128, 0:16] = part[:, 384:400]

    lane = iota((8, 128), 1)
    upper = iota((8, 128), 0) < 4

    def one_w(w, carry):
        loaded = {}

        def load(r, j):
            if (r, j) not in loaded:
                loaded[(r, j)] = y_ref[j, pl.ds(w * 32 + r, 8, stride=YS), :]
            return loaded[(r, j)]

        def chunk(e, i):
            first = 5000 * e + 128 * i
            count = min(128, 5000 - 128 * i)
            done = 0
            value = None
            while done < count:
                r, o = divmod(first + done, 400)
                j, s = divmod(o, 128)
                n = min(128 - s, 400 - o, count - done)
                shift = (done - s) % 128
                piece = load(r, j)
                if shift:
                    piece = pltpu.roll(piece, shift, 1)
                value = piece if value is None else jnp.where(lane < done, value, piece)
                done += n
            if count < 128:
                value = jnp.where(lane < count, value, 0.0)
            return value

        for e in range(2):
            for k in range(NK):
                x0 = chunk(e, 2 * k)
                x1 = chunk(e, 2 * k + 1)
                f_ref[4 * w + e, 8 * k : 8 * k + 8, :] = jnp.where(upper, x0, pltpu.roll(x1, 4, 0))
                f_ref[4 * w + 2 + e, 8 * k : 8 * k + 8, :] = jnp.where(upper, pltpu.roll(x0, 4, 0), x1)
        return carry

    lax.fori_loop(0, 4, one_w, 0)


def backward_kernel(d_ref, c_ref, a_ref, o_ref, h_ref, ap_ref, y_ref):
    pad_latitude(a_ref, ap_ref)
    y_ref[...] = jnp.zeros_like(y_ref)
    lane = iota((8, 128), 1)
    upper = iota((8, 128), 0) < 4

    def one_w(w, carry):
        chunks = {}

        def chunk(e, i):
            if (e, i) not in chunks:
                k = i // 2
                t0 = d_ref[4 * w + e, 8 * k : 8 * k + 8, :]
                t1 = d_ref[4 * w + 2 + e, 8 * k : 8 * k + 8, :]
                chunks[(e, 2 * k)] = jnp.where(upper, t0, pltpu.roll(t1, 4, 0))
                chunks[(e, 2 * k + 1)] = jnp.where(upper, pltpu.roll(t0, 4, 0), t1)
            return chunks[(e, i)]

        for r in range(25):
            for j in range(4):
                first = 400 * r + 128 * j
                count = min(128, 400 - 128 * j)
                done = 0
                value = None
                while done < count:
                    e, c = divmod(first + done, 5000)
                    i, s = divmod(c, 128)
                    n = min(128 - s, 5000 - c, count - done)
                    shift = (done - s) % 128
                    piece = chunk(e, i)
                    if shift:
                        piece = pltpu.roll(piece, shift, 1)
                    value = piece if value is None else jnp.where(lane < done, value, piece)
                    done += n
                y_ref[j, pl.ds(w * 32 + r, 8, stride=YS), :] = value
        return carry

    lax.fori_loop(0, 4, one_w, 0)
    lat = split(ap_ref[...])
    lon = split(o_ref[...])
    for l in range(4):
        field = jnp.concatenate(
            [
                jnp.concatenate([y_ref[j, (4 * u + l) * YS : (4 * u + l) * YS + 128, :] for j in range(4)], axis=1)
                for u in range(2)
            ],
            axis=0,
        )
        rows = mm3(lat, split(field), TN)
        h_ref[l] = c_ref[l] + mm3(split(rows[:, :400]), lon)


def prepare_kernel(kf_ref, kl_ref, s_ref, key_ref, p_ref, v_ref, spk_ref, vb_ref, vt_ref, pp_ref):
    take = [
        (((iota((64, 128), 1) // 8) * 4 + iota((64, 128), 1) % 4 == iota((64, 128), 0)) & ((iota((64, 128), 1) // 4) % 2 == p))
        .astype(F32)
        .astype(BF16)
        for p in range(2)
    ]
    put = [(iota((128, 64), 0) == iota((128, 64), 1) + 64 * p).astype(F32).astype(BF16) for p in range(2)]
    for n, v in enumerate(split(v_ref[...])):
        big = jnp.zeros((128, 128), F32)
        for p in range(2):
            wide = mm(v, take[p], NN).astype(BF16)
            big = big + mm(put[p], wide, NN)
        vb_ref[n] = big.astype(BF16)
        vt_ref[n] = big.T.astype(BF16)

    pp_ref[:, 0:4992] = p_ref[:, 0:4992]
    pp_ref[:, 4992:5120] = jnp.zeros((256, 128), BF16)
    pp_ref[:, 4992:5000] = p_ref[:, 4992:5000]
    scale = s_ref[0]

    def one_block(b, carry):
        key = key_ref[pl.ds(b, 1), :]
        cell = key >> 8
        mine = iota((256, OB), 0) == (key & 255)
        first = jnp.minimum(kf_ref[b], NK - 2)

        def window(k, width):
            start = pl.multiple_of(k * 256, 256)
            hot = (iota((width, OB), 0) == cell - start).astype(F32).astype(BF16)
            z = mm(pp_ref[:, pl.ds(start, width)], hot, NN)
            return jnp.sum(jnp.where(mine, z, 0.0), axis=0, keepdims=True)

        total = window(first, 512)
        total = lax.fori_loop(first + 2, kl_ref[b] + 1, lambda k, t: t + window(k, 256), total)
        spk_ref[pl.ds(b, 1), :] = total * scale
        return carry

    lax.fori_loop(0, NB, one_block, 0)


def obs_parts(key, first):
    cell = (key >> 8) - first * 256
    row = ((cell >> 7) & 1) * 64 + (key & 63)
    inside = cell >= 0
    at = jnp.where(inside, (cell >> 8) * 128 + (cell & 127), -1)
    return row, at


def observe_kernel(kf_ref, kl_ref, key_ref, spk_ref, vb_ref, r_ref, out_ref, l_ref, part_ref):
    vb = (vb_ref[0], vb_ref[1])
    for k in range(NK):
        h = r_ref[:, 8 * k : 8 * k + 8, :].reshape(128, 128)
        hi, lo = split(mm3(vb, split(h)))
        l_ref[k, :, 0:128] = hi
        l_ref[k, :, 128:256] = lo

    def one_block(b, carry):
        key = key_ref[pl.ds(b, 1), :]
        first = jnp.minimum(kf_ref[b], NK - 2)
        row, at = obs_parts(key, first)
        mine = iota((128, OB), 0) == row
        hot = (iota((256, OB), 0) == at).astype(F32).astype(BF16)
        h0, h1 = hot[0:128], hot[128:256]
        z = mm(l_ref[first], jnp.concatenate([h0, h0], axis=0), NN)
        z = z + mm(l_ref[first + 1], jnp.concatenate([h1, h1], axis=0), NN)
        total = jnp.sum(jnp.where(mine, z, 0.0), axis=0, keepdims=True)

        def more(k, t):
            at_k = at - (k - first) * 128
            hk = (iota((128, OB), 0) == at_k).astype(F32).astype(BF16)
            zk = mm(l_ref[k], jnp.concatenate([hk, hk], axis=0), NN)
            return t + jnp.sum(jnp.where(mine, zk, 0.0), axis=0, keepdims=True)

        total = lax.fori_loop(first + 2, kl_ref[b] + 1, more, total)
        part_ref[pl.ds(b, 1), :] = total
        return carry

    lax.fori_loop(0, NB, one_block, 0)
    out_ref[...] = jnp.broadcast_to((part_ref[...] * spk_ref[...])[None], out_ref.shape)


def adjoint_kernel(kf_ref, kl_ref, key_ref, spk_ref, w_ref, ag_ref, vt_ref, d_ref, adj_ref, u_ref):
    adj_ref[...] = jnp.zeros_like(adj_ref)
    u_ref[...] = spk_ref[...] * (w_ref[...] * jnp.sum(ag_ref[...], axis=0))

    def one_block(b, carry):
        key = key_ref[pl.ds(b, 1), :]
        first = jnp.minimum(kf_ref[b], NK - 2)
        row, at = obs_parts(key, first)
        mine = iota((128, OB), 0) == row
        u = u_ref[pl.ds(b, 1), :]
        uh = u.astype(BF16).astype(F32)
        parts = [jnp.where(mine, x, 0.0).astype(BF16) for x in (uh, u - uh)]
        hot = (iota((256, OB), 0) == at).astype(F32).astype(BF16)
        z = mm(parts[0], hot, NT) + mm(parts[1], hot, NT)
        adj_ref[first] += z[:, 0:128]
        adj_ref[first + 1] += z[:, 128:256]

        def more(k, c):
            at_k = at - (k - first) * 128
            hk = (iota((128, OB), 0) == at_k).astype(F32).astype(BF16)
            adj_ref[k] += mm(parts[0], hk, NT) + mm(parts[1], hk, NT)
            return c

        return lax.fori_loop(first + 2, kl_ref[b] + 1, more, carry)

    lax.fori_loop(0, NB, one_block, 0)
    vt = (vt_ref[0], vt_ref[1])
    for k in range(NK):
        d_ref[:, 8 * k : 8 * k + 8, :] = mm3(vt, split(adj_ref[k])).reshape(16, 8, 128)


VM = pl.BlockSpec(memory_space=pltpu.VMEM)
SM = pl.BlockSpec(memory_space=pltpu.SMEM)


def call(kernel, outs, ins, scratch, flops, nbytes, name):
    return pl.pallas_call(
        kernel,
        out_shape=outs,
        in_specs=ins,
        out_specs=jax.tree.map(lambda _: VM, outs),
        scratch_shapes=scratch,
        compiler_params=pltpu.CompilerParams(vmem_limit_bytes=48 * 1024 * 1024),
        cost_estimate=pl.CostEstimate(flops=flops, bytes_accessed=nbytes, transcendentals=0),
        name=name,
    )


def body(
    control,
    perturbations,
    member_scales,
    vertical_loc,
    latitude_loc,
    longitude_loc,
    observed_index,
    observed_weight,
):
    sds = jax.ShapeDtypeStruct
    field_scratch = [pltpu.VMEM((256, 200), F32), pltpu.VMEM((4, 8 * YS, 128), F32)]
    c = control[0]
    flat = call(
        forward_kernel, sds((16, 160, 128), F32), [VM] * 3, field_scratch, 3_000_000_000, 4_000_000, "forward"
    )(c, latitude_loc, longitude_loc)
    columns = lax.all_to_all(flat, "lev", split_axis=0, concat_axis=0, tiled=True)

    slot = jnp.arange(2, dtype=I32)[:, None] * 128
    cell = observed_index % 5000
    key = cell * 256 + slot + observed_index // 5000
    key, weight = lax.sort((key.reshape(8192), observed_weight.reshape(8192)), num_keys=1)
    key = key.reshape(NB, OB)
    weight = weight.reshape(NB, OB)
    kf = key[:, 0] >> 16
    kl = key[:, OB - 1] >> 16
    spk, vb, vt = call(
        prepare_kernel,
        (sds((NB, OB), F32), sds((2, 128, 128), BF16), sds((2, 128, 128), BF16)),
        [SM, SM, SM, VM, VM, VM],
        [pltpu.VMEM((256, 5120), BF16)],
        4_000_000_000,
        3_000_000,
        "prepare",
    )(kf, kl, member_scales, key, perturbations.reshape(256, 5000), vertical_loc)

    copies = call(
        observe_kernel,
        sds((8, NB, OB), F32),
        [SM, SM, VM, VM, VM, VM],
        [pltpu.VMEM((NK, 128, 256), BF16), pltpu.VMEM((NB, OB), F32)],
        3_000_000_000,
        2_000_000,
        "observe",
    )(kf, kl, key, spk, vb, columns)
    gathered = lax.all_to_all(copies, "mem", split_axis=0, concat_axis=0, tiled=True)
    adjoint = call(
        adjoint_kernel,
        sds((16, 160, 128), F32),
        [SM, SM, VM, VM, VM, VM, VM],
        [pltpu.VMEM((NK, 128, 128), F32), pltpu.VMEM((NB, OB), F32)],
        3_000_000_000,
        2_000_000,
        "adjoint",
    )(kf, kl, key, spk, weight, gathered, vt)
    levels = lax.all_to_all(adjoint, "lev", split_axis=0, concat_axis=0, tiled=True)
    result = call(
        backward_kernel, sds((4, 200, 400), F32), [VM] * 4, field_scratch, 3_000_000_000, 5_000_000, "backward"
    )(levels, c, latitude_loc, longitude_loc)
    return result[None]


def solution(mesh):
    placed = (
        P("mem", "lev", None, None),
        P("mem", None, None, None, "lev"),
        P("mem"),
        P(),
        P(),
        P(),
        P(None, "lev"),
        P(None, "lev"),
    )
    return jax.shard_map(
        body, mesh=mesh, in_specs=placed, out_specs=P("mem", "lev", None, None), check_vma=False
    )
```

```python
import functools

import jax
import jax.numpy as jnp
from jax import lax
from jax.experimental import pallas as pl
from jax.experimental.pallas import tpu as pltpu
from jax.sharding import PartitionSpec as P

F32 = jnp.float32
BF16 = jnp.bfloat16
I32 = jnp.int32

NB = 32
OB = 256
NK = 20
YS = 136
NN = (((1,), (0,)), ((), ()))
NT = (((1,), (1,)), ((), ()))
TN = (((0,), (0,)), ((), ()))


def split(x):
    hi = x.astype(BF16)
    return hi, (x - hi.astype(F32)).astype(BF16)


def mm(a, b, dims):
    return lax.dot_general(a, b, dims, preferred_element_type=F32)


def mm3(a, b, dims=NN):
    return mm(a[0], b[0], dims) + (mm(a[0], b[1], dims) + mm(a[1], b[0], dims))


def pad_latitude(a_ref, ap_ref):
    ap_ref[...] = jnp.zeros_like(ap_ref)
    for i in range(8):
        row = (i % 2) * 128 + (i // 2) * 32
        ap_ref[row : row + 25, :] = a_ref[25 * i : 25 * i + 25, :]


def iota(shape, dim):
    return lax.broadcasted_iota(I32, shape, dim)


def forward_kernel(c_hbm, a_hbm, o_hbm, f_ref, lat_ref, lon_ref, ap_ref, y_ref, c_ref, a_ref, o_ref, sem):
    copies = [pltpu.make_async_copy(o_hbm, o_ref, sem.at[0])]
    copies += [pltpu.make_async_copy(c_hbm.at[l], c_ref.at[l], sem.at[2 + l]) for l in range(4)]
    copies.insert(2, pltpu.make_async_copy(a_hbm, a_ref, sem.at[1]))
    for copy in copies:
        copy.start()
    copies[0].wait()
    lon = split(o_ref[...])
    lon_ref[0], lon_ref[1] = lon
    copies[1].wait()
    rows = mm3(split(c_ref[0]), lon, NT)
    copies[2].wait()
    pad_latitude(a_ref, ap_ref)
    lat = split(ap_ref[...])
    lat_ref[0], lat_ref[1] = lat
    for l in range(4):
        if l:
            copies[2 + l].wait()
            rows = mm3(split(c_ref[l]), lon, NT)
        field = mm3(lat, split(rows))
        for u in range(2):
            base = (4 * u + l) * YS
            part = field[128 * u : 128 * u + 128]
            for j in range(3):
                y_ref[j, base : base + 128, :] = part[:, 128 * j : 128 * j + 128]
            y_ref[3, base : base + 128, 0:16] = part[:, 384:400]

    lane = iota((8, 128), 1)
    upper = iota((8, 128), 0) < 4

    def one_w(w, carry):
        loaded = {}

        def load(r, j):
            if (r, j) not in loaded:
                loaded[(r, j)] = y_ref[j, pl.ds(w * 32 + r, 8, stride=YS), :]
            return loaded[(r, j)]

        def chunk(e, i):
            first = 5000 * e + 128 * i
            count = min(128, 5000 - 128 * i)
            done = 0
            value = None
            while done < count:
                r, o = divmod(first + done, 400)
                j, s = divmod(o, 128)
                n = min(128 - s, 400 - o, count - done)
                shift = (done - s) % 128
                piece = load(r, j)
                if shift:
                    piece = pltpu.roll(piece, shift, 1)
                value = piece if value is None else jnp.where(lane < done, value, piece)
                done += n
            if count < 128:
                value = jnp.where(lane < count, value, 0.0)
            return value

        for e in range(2):
            for k in range(NK):
                x0 = chunk(e, 2 * k)
                x1 = chunk(e, 2 * k + 1)
                f_ref[4 * w + e, 8 * k : 8 * k + 8, :] = jnp.where(upper, x0, pltpu.roll(x1, 4, 0))
                f_ref[4 * w + 2 + e, 8 * k : 8 * k + 8, :] = jnp.where(upper, pltpu.roll(x0, 4, 0), x1)
        return carry

    lax.fori_loop(0, 4, one_w, 0)


def backward_kernel(d_ref, c_ref, lat_ref, lon_ref, h_ref, y_ref):
    for j in range(4):
        for g in range(8):
            for w in range(4):
                row = g * YS + w * 32 + 25
                y_ref[j, row : row + 7, :] = jnp.zeros((7, 128), F32)
    lane = iota((8, 128), 1)
    upper = iota((8, 128), 0) < 4

    def one_w(w, carry):
        chunks = {}

        def chunk(e, i):
            if (e, i) not in chunks:
                k = i // 2
                t0 = d_ref[4 * w + e, 8 * k : 8 * k + 8, :]
                t1 = d_ref[4 * w + 2 + e, 8 * k : 8 * k + 8, :]
                chunks[(e, 2 * k)] = jnp.where(upper, t0, pltpu.roll(t1, 4, 0))
                chunks[(e, 2 * k + 1)] = jnp.where(upper, pltpu.roll(t0, 4, 0), t1)
            return chunks[(e, i)]

        for r in range(25):
            for j in range(4):
                first = 400 * r + 128 * j
                count = min(128, 400 - 128 * j)
                done = 0
                value = None
                while done < count:
                    e, c = divmod(first + done, 5000)
                    i, s = divmod(c, 128)
                    n = min(128 - s, 5000 - c, count - done)
                    shift = (done - s) % 128
                    piece = chunk(e, i)
                    if shift:
                        piece = pltpu.roll(piece, shift, 1)
                    value = piece if value is None else jnp.where(lane < done, value, piece)
                    done += n
                y_ref[j, pl.ds(w * 32 + r, 8, stride=YS), :] = value
        return carry

    lax.fori_loop(0, 4, one_w, 0)
    lat = (lat_ref[0], lat_ref[1])
    lon = (lon_ref[0], lon_ref[1])
    for l in range(4):
        field = jnp.concatenate(
            [
                jnp.concatenate([y_ref[j, (4 * u + l) * YS : (4 * u + l) * YS + 128, :] for j in range(4)], axis=1)
                for u in range(2)
            ],
            axis=0,
        )
        rows = mm3(lat, split(field), TN)
        h_ref[l] = c_ref[l] + mm3(split(rows[:, :400]), lon)


def obs_parts(key, first):
    cell = (key >> 8) - first * 256
    row = ((cell >> 7) & 1) * 64 + (key & 63)
    return row, (cell >> 8) * 128 + (cell & 127)


def index_rows():
    return iota((256, OB), 0).astype(F32).astype(BF16)


def one_hot(index, at, width):
    return jnp.where(index[0:width] == at.astype(F32).astype(BF16), jnp.ones((), BF16), jnp.zeros((), BF16))


def pick(mask, z):
    return jnp.sum(jnp.where(mask, z, 0.0), axis=0, keepdims=True)


def prepare_kernel(kf_ref, kl_ref, s_ref, key_ref, p_hbm, v_ref, spk_ref, vb_ref, vt_ref, more_ref, p_ref, pp_ref, sem):
    copy = pltpu.make_async_copy(p_hbm, p_ref, sem)
    copy.start()
    take = [
        (((iota((64, 128), 1) // 8) * 4 + iota((64, 128), 1) % 4 == iota((64, 128), 0)) & ((iota((64, 128), 1) // 4) % 2 == p))
        .astype(F32)
        .astype(BF16)
        for p in range(2)
    ]
    put = [(iota((128, 64), 0) == iota((128, 64), 1) + 64 * p).astype(F32).astype(BF16) for p in range(2)]
    for n, v in enumerate(split(v_ref[...])):
        big = jnp.zeros((128, 128), F32)
        for p in range(2):
            wide = mm(v, take[p], NN).astype(BF16)
            big = big + mm(put[p], wide, NN)
        vb_ref[n] = big.astype(BF16)
        vt_ref[n] = big.T.astype(BF16)

    def one_span(b, t):
        return jnp.maximum(t, kl_ref[b] - jnp.minimum(kf_ref[b], NK - 2))

    more = lax.fori_loop(0, NB, one_span, 0, unroll=True)
    more_ref[0] = more

    copy.wait()
    for i in range(2 * NK - 1):
        pp_ref[i % 2, :, 128 * (i // 2) : 128 * (i // 2) + 128] = p_ref[:, 128 * i : 128 * i + 128]
    pp_ref[1, :, 2432:2560] = jnp.zeros((256, 128), BF16)
    pp_ref[1, :, 2432:2440] = p_ref[:, 4992:5000]
    scale = s_ref[0]
    rows = iota((256, OB), 0)
    index = index_rows()

    def select(key, start, width, hot):
        half = (key >> 15) & 1
        mine = key & 255
        lanes = pl.ds(pl.multiple_of(start * 128, 128), width)
        z = [mm(pp_ref[p, :, lanes], hot, NN) for p in range(2)]
        return pick(rows == mine, jnp.where(half == 0, z[0], z[1]))

    def one_block(b, carry):
        key = key_ref[pl.ds(b, 1), :]
        first = jnp.minimum(kf_ref[b], NK - 2)
        _, at = obs_parts(key, first)
        spk_ref[pl.ds(b, 1), :] = select(key, first, 256, one_hot(index, at, 256)) * scale
        return carry

    lax.fori_loop(0, NB, one_block, 0, unroll=4)

    @pl.when(more > 1)
    def _():
        def one_more(b, carry):
            key = key_ref[pl.ds(b, 1), :]
            first = jnp.minimum(kf_ref[b], NK - 2)

            def window(k, t):
                _, at = obs_parts(key, k)
                return t + select(key, k, 128, one_hot(index, at, 128)) * scale

            spk_ref[pl.ds(b, 1), :] = lax.fori_loop(first + 2, kl_ref[b] + 1, window, spk_ref[pl.ds(b, 1), :])
            return carry

        lax.fori_loop(0, NB, one_more, 0)


def observe_kernel(kf_ref, kl_ref, more_ref, key_ref, spk_ref, vb_ref, r_ref, out_ref, l_ref, part_ref):
    vh, vl = vb_ref[0], vb_ref[1]
    v1 = jnp.concatenate([vh, vl], axis=1)
    for k in range(0, NK, 2):
        h = [r_ref[:, 8 * (k + n) : 8 * (k + n) + 8, :].reshape(128, 128) for n in range(2)]
        hh, hl = split(jnp.concatenate(h, axis=1))
        field = mm(v1, jnp.concatenate([hh, hh], axis=0), NN) + mm(vh, hl, NN)
        hi, lo = split(field)
        l_ref[0:128, 128 * k : 128 * k + 256] = hi
        l_ref[128:256, 128 * k : 128 * k + 256] = lo
    rows = iota((128, OB), 0)
    index = index_rows()

    def value(row, start, width, hot):
        z = mm(l_ref[:, pl.ds(pl.multiple_of(start * 128, 128), width)], hot, NN)
        return pick(rows == row, z[0:128] + z[128:256])

    def one_block(b, carry):
        key = key_ref[pl.ds(b, 1), :]
        first = jnp.minimum(kf_ref[b], NK - 2)
        row, at = obs_parts(key, first)
        part_ref[pl.ds(b, 1), :] = value(row, first, 256, one_hot(index, at, 256))
        return carry

    lax.fori_loop(0, NB, one_block, 0, unroll=4)

    @pl.when(more_ref[0] > 1)
    def _():
        def one_more(b, carry):
            key = key_ref[pl.ds(b, 1), :]
            first = jnp.minimum(kf_ref[b], NK - 2)

            def window(k, t):
                row, at = obs_parts(key, k)
                return t + value(row, k, 128, one_hot(index, at, 128))

            part_ref[pl.ds(b, 1), :] = lax.fori_loop(first + 2, kl_ref[b] + 1, window, part_ref[pl.ds(b, 1), :])
            return carry

        lax.fori_loop(0, NB, one_more, 0)

    out_ref[...] = jnp.broadcast_to((part_ref[...] * spk_ref[...])[None], out_ref.shape)


def adjoint_kernel(kf_ref, kl_ref, more_ref, key_ref, spk_ref, w_ref, vt_ref, ag_ref, d_ref, adj_ref, u_ref):
    adj_ref[...] = jnp.zeros_like(adj_ref)
    u_ref[...] = spk_ref[...] * (w_ref[...] * jnp.sum(ag_ref[...], axis=0))
    index = index_rows()

    def add(row, u, start, width, hot):
        mine = index[0:128] == row.astype(F32).astype(BF16)
        parts = [jnp.where(mine, x, jnp.zeros((), BF16)) for x in split(u)]
        z = mm(jnp.concatenate(parts, axis=0), hot, NT)
        adj_ref[:, pl.ds(pl.multiple_of(start * 128, 128), width)] += z[0:128] + z[128:256]

    def one_block(b, carry):
        key = key_ref[pl.ds(b, 1), :]
        first = jnp.minimum(kf_ref[b], NK - 2)
        row, at = obs_parts(key, first)
        add(row, u_ref[pl.ds(b, 1), :], first, 256, one_hot(index, at, 256))
        return carry

    lax.fori_loop(0, NB, one_block, 0, unroll=4)

    @pl.when(more_ref[0] > 1)
    def _():
        def one_more(b, carry):
            key = key_ref[pl.ds(b, 1), :]
            first = jnp.minimum(kf_ref[b], NK - 2)

            def window(k, c):
                row, at = obs_parts(key, k)
                add(row, u_ref[pl.ds(b, 1), :], k, 128, one_hot(index, at, 128))
                return c

            return lax.fori_loop(first + 2, kl_ref[b] + 1, window, carry)

        lax.fori_loop(0, NB, one_more, 0)

    th, tl = vt_ref[0], vt_ref[1]
    t1 = jnp.concatenate([th, tl], axis=1)
    for k in range(0, NK, 2):
        ah, al = split(adj_ref[:, 128 * k : 128 * k + 256])
        d = mm(t1, jnp.concatenate([ah, ah], axis=0), NN) + mm(th, al, NN)
        for n in range(2):
            d_ref[:, 8 * (k + n) : 8 * (k + n) + 8, :] = d[:, 128 * n : 128 * n + 128].reshape(16, 8, 128)


VM = pl.BlockSpec(memory_space=pltpu.VMEM)
SM = pl.BlockSpec(memory_space=pltpu.SMEM)
HB = pl.BlockSpec(memory_space=pltpu.HBM)
DMA = pltpu.SemaphoreType.DMA


def call(kernel, outs, ins, scratch, flops, nbytes, kib, name, out_specs=None):
    return pl.pallas_call(
        kernel,
        out_shape=outs,
        in_specs=ins,
        out_specs=out_specs or jax.tree.map(lambda _: VM, outs),
        scratch_shapes=scratch,
        compiler_params=pltpu.CompilerParams(vmem_limit_bytes=kib * 1024),
        cost_estimate=pl.CostEstimate(flops=flops, bytes_accessed=nbytes, transcendentals=0),
        name=name,
    )


def body(
    control,
    perturbations,
    member_scales,
    vertical_loc,
    latitude_loc,
    longitude_loc,
    observed_index,
    observed_weight,
):
    sds = jax.ShapeDtypeStruct
    rows_scratch = pltpu.VMEM((4, 8 * YS, 128), F32)
    c = control[0]
    flat, lat, lon = call(
        forward_kernel,
        (sds((16, 160, 128), F32), sds((2, 256, 200), BF16), sds((2, 400, 400), BF16)),
        [HB] * 3,
        [
            pltpu.VMEM((256, 200), F32),
            rows_scratch,
            pltpu.VMEM((4, 200, 400), F32),
            pltpu.VMEM((200, 200), F32),
            pltpu.VMEM((400, 400), F32),
            DMA((6,)),
        ],
        3_000_000_000,
        4_000_000,
        65400,
        "forward",
    )(c, latitude_loc, longitude_loc)
    columns = lax.all_to_all(flat, "lev", split_axis=0, concat_axis=0, tiled=True)

    slot = jnp.arange(2, dtype=I32)[:, None] * 128
    cell = observed_index % 5000
    key = cell * 256 + slot + observed_index // 5000
    key, weight = lax.sort((key.reshape(8192), observed_weight.reshape(8192)), num_keys=1)
    key = key.reshape(NB, OB)
    weight = weight.reshape(NB, OB)
    kf = key[:, 0] >> 16
    kl = key[:, OB - 1] >> 16
    spk, vb, vt, more = call(
        prepare_kernel,
        (
            sds((NB, OB), F32),
            sds((2, 128, 128), BF16),
            sds((2, 128, 128), BF16),
            sds((1,), I32),
        ),
        [SM, SM, SM, VM, HB, VM],
        [pltpu.VMEM((256, 5000), BF16), pltpu.VMEM((2, 256, 2560), BF16), DMA(())],
        4_000_000_000,
        3_000_000,
        64512,
        "prepare",
        (VM, VM, VM, SM),
    )(kf, kl, member_scales, key, perturbations.reshape(256, 5000), vertical_loc)

    copies = call(
        observe_kernel,
        sds((8, NB, OB), F32),
        [SM, SM, SM, VM, VM, VM, VM],
        [pltpu.VMEM((256, NK * 128), BF16), pltpu.VMEM((NB, OB), F32)],
        3_000_000_000,
        2_000_000,
        62464,
        "observe",
    )(kf, kl, more, key, spk, vb, columns)
    gathered = lax.all_to_all(copies, "mem", split_axis=0, concat_axis=0, tiled=True)
    adjoint = call(
        adjoint_kernel,
        sds((16, 160, 128), F32),
        [SM, SM, SM, VM, VM, VM, VM, VM],
        [pltpu.VMEM((128, NK * 128), F32), pltpu.VMEM((NB, OB), F32)],
        3_000_000_000,
        2_000_000,
        24576,
        "adjoint",
    )(kf, kl, more, key, spk, weight, vt, gathered)
    levels = lax.all_to_all(adjoint, "lev", split_axis=0, concat_axis=0, tiled=True)
    result = call(
        backward_kernel, sds((4, 200, 400), F32), [VM] * 4, [rows_scratch], 3_000_000_000, 5_000_000, 24_576, "backward"
    )(levels, c, lat, lon)
    return result[None]


def solution(mesh):
    placed = (
        P("mem", "lev", None, None),
        P("mem", None, None, None, "lev"),
        P("mem"),
        P(),
        P(),
        P(),
        P(None, "lev"),
        P(None, "lev"),
    )
    return jax.shard_map(
        body, mesh=mesh, in_specs=placed, out_specs=P("mem", "lev", None, None), check_vma=False
    )
```

```python
import functools

import jax
import jax.numpy as jnp
from jax import lax
from jax.experimental import pallas as pl
from jax.experimental.pallas import tpu as pltpu
from jax.sharding import PartitionSpec as P

F32 = jnp.float32
BF16 = jnp.bfloat16
I32 = jnp.int32

NB = 32
OB = 256
NK = 20
YS = 136
NN = (((1,), (0,)), ((), ()))
NT = (((1,), (1,)), ((), ()))
TN = (((0,), (0,)), ((), ()))


def split(x):
    hi = x.astype(BF16)
    return hi, (x - hi.astype(F32)).astype(BF16)


def mm(a, b, dims):
    return lax.dot_general(a, b, dims, preferred_element_type=F32)


def mm3(a, b, dims=NN):
    return mm(a[0], b[0], dims) + (mm(a[0], b[1], dims) + mm(a[1], b[0], dims))


def pad_latitude(a_ref, ap_ref):
    ap_ref[...] = jnp.zeros_like(ap_ref)
    for i in range(8):
        row = (i % 2) * 128 + (i // 2) * 32
        ap_ref[row : row + 25, :] = a_ref[25 * i : 25 * i + 25, :]


def iota(shape, dim):
    return lax.broadcasted_iota(I32, shape, dim)


def forward_kernel(c_hbm, a_hbm, o_hbm, f_hbm, f_ref, y_ref, c_ref, a_ref, o_ref, sem, out_sem):
    reads = [
        pltpu.make_async_copy(a_hbm, a_ref, sem.at[0]),
        pltpu.make_async_copy(c_hbm, c_ref, sem.at[1]),
        pltpu.make_async_copy(o_hbm, o_ref, sem.at[2]),
    ]
    for copy in reads:
        copy.start()
    reads[0].wait()
    reads[1].wait()
    lat = split(a_ref[...])
    rows = [split(mm3(lat, split(c_ref[l]))) for l in range(4)]
    reads[2].wait()
    lon = split(o_ref[...])
    for l in range(4):
        field = mm3(rows[l], lon, NT)
        for i in range(8):
            row = (4 * (i % 2) + l) * YS + 32 * (i // 2)
            part = field[25 * i : 25 * i + 25]
            for j in range(3):
                y_ref[j, row : row + 25, :] = part[:, 128 * j : 128 * j + 128]
            y_ref[3, row : row + 25, 0:16] = part[:, 384:400]

    lane = iota((8, 128), 1)
    upper = iota((8, 128), 0) < 4

    def write(w):
        blocks = pl.ds(4 * w, 4)
        return pltpu.make_async_copy(f_ref.at[blocks], f_hbm.at[blocks], out_sem.at[w])

    def one_w(w, carry):
        loaded = {}

        def load(r, j):
            if (r, j) not in loaded:
                loaded[(r, j)] = y_ref[j, pl.ds(w * 32 + r, 8, stride=YS), :]
            return loaded[(r, j)]

        def chunk(e, i):
            first = 5000 * e + 128 * i
            count = min(128, 5000 - 128 * i)
            done = 0
            value = None
            while done < count:
                r, o = divmod(first + done, 400)
                j, s = divmod(o, 128)
                n = min(128 - s, 400 - o, count - done)
                shift = (done - s) % 128
                piece = load(r, j)
                if shift:
                    piece = pltpu.roll(piece, shift, 1)
                value = piece if value is None else jnp.where(lane < done, value, piece)
                done += n
            if count < 128:
                value = jnp.where(lane < count, value, 0.0)
            return value

        for e in range(2):
            for k in range(NK):
                x0 = chunk(e, 2 * k)
                x1 = chunk(e, 2 * k + 1)
                f_ref[4 * w + e, 8 * k : 8 * k + 8, :] = jnp.where(upper, x0, pltpu.roll(x1, 4, 0))
                f_ref[4 * w + 2 + e, 8 * k : 8 * k + 8, :] = jnp.where(upper, pltpu.roll(x0, 4, 0), x1)
        write(w).start()
        return carry

    lax.fori_loop(0, 4, one_w, 0)
    for w in range(4):
        write(w).wait()


def backward_kernel(d_ref, c_ref, lat_ref, lon_ref, h_hbm, y_ref, h_ref, sem):
    for j in range(4):
        for g in range(8):
            for w in range(4):
                row = g * YS + w * 32 + 25
                y_ref[j, row : row + 7, :] = jnp.zeros((7, 128), F32)
    lane = iota((8, 128), 1)
    upper = iota((8, 128), 0) < 4

    def one_w(w, carry):
        chunks = {}

        def chunk(e, i):
            if (e, i) not in chunks:
                k = i // 2
                t0 = d_ref[4 * w + e, 8 * k : 8 * k + 8, :]
                t1 = d_ref[4 * w + 2 + e, 8 * k : 8 * k + 8, :]
                chunks[(e, 2 * k)] = jnp.where(upper, t0, pltpu.roll(t1, 4, 0))
                chunks[(e, 2 * k + 1)] = jnp.where(upper, pltpu.roll(t0, 4, 0), t1)
            return chunks[(e, i)]

        for r in range(25):
            for j in range(4):
                first = 400 * r + 128 * j
                count = min(128, 400 - 128 * j)
                done = 0
                value = None
                while done < count:
                    e, c = divmod(first + done, 5000)
                    i, s = divmod(c, 128)
                    n = min(128 - s, 5000 - c, count - done)
                    shift = (done - s) % 128
                    piece = chunk(e, i)
                    if shift:
                        piece = pltpu.roll(piece, shift, 1)
                    value = piece if value is None else jnp.where(lane < done, value, piece)
                    done += n
                y_ref[j, pl.ds(w * 32 + r, 8, stride=YS), :] = value
        return carry

    lax.fori_loop(0, 4, one_w, 0)
    writes = []
    lat = (lat_ref[0], lat_ref[1])
    lon = (lon_ref[0], lon_ref[1])
    for l in range(4):
        field = jnp.concatenate(
            [
                jnp.concatenate([y_ref[j, (4 * u + l) * YS : (4 * u + l) * YS + 128, :] for j in range(4)], axis=1)
                for u in range(2)
            ],
            axis=0,
        )
        rows = mm3(lat, split(field), TN)
        h_ref[l] = c_ref[l] + mm3(split(rows[:, :400]), lon)
        writes.append(pltpu.make_async_copy(h_ref.at[l], h_hbm.at[l], sem.at[l]))
        writes[l].start()
    for copy in writes:
        copy.wait()


def obs_parts(key, first):
    cell = (key >> 8) - first * 256
    row = ((cell >> 7) & 1) * 64 + (key & 63)
    return row, (cell >> 8) * 128 + (cell & 127)


def index_rows():
    return iota((256, OB), 0).astype(F32).astype(BF16)


def one_hot(index, at, width):
    return jnp.where(index[0:width] == at.astype(F32).astype(BF16), jnp.ones((), BF16), jnp.zeros((), BF16))


def pick(mask, z):
    return jnp.sum(jnp.where(mask, z, 0.0), axis=0, keepdims=True)


def prepare_kernel(
    kf_ref, kl_ref, s_ref, key_ref, p_hbm, v_ref, spk_ref, vb_ref, vt_ref, more_ref, p_ref, pp_ref, sem
):
    copy = pltpu.make_async_copy(p_hbm, p_ref, sem)
    copy.start()
    take = [
        (((iota((64, 128), 1) // 8) * 4 + iota((64, 128), 1) % 4 == iota((64, 128), 0)) & ((iota((64, 128), 1) // 4) % 2 == p))
        .astype(F32)
        .astype(BF16)
        for p in range(2)
    ]
    put = [(iota((128, 64), 0) == iota((128, 64), 1) + 64 * p).astype(F32).astype(BF16) for p in range(2)]
    for n, v in enumerate(split(v_ref[...])):
        big = jnp.zeros((128, 128), F32)
        for p in range(2):
            wide = mm(v, take[p], NN).astype(BF16)
            big = big + mm(put[p], wide, NN)
        vb_ref[n] = big.astype(BF16)
        vt_ref[n] = big.T.astype(BF16)

    def one_span(b, t):
        return jnp.maximum(t, kl_ref[b] - jnp.minimum(kf_ref[b], NK - 2))

    more = lax.fori_loop(0, NB, one_span, 0, unroll=True)
    more_ref[0] = more

    copy.wait()
    for i in range(2 * NK - 1):
        pp_ref[i % 2, :, 128 * (i // 2) : 128 * (i // 2) + 128] = p_ref[:, 128 * i : 128 * i + 128]
    pp_ref[1, :, 2432:2560] = jnp.zeros((256, 128), BF16)
    pp_ref[1, :, 2432:2440] = p_ref[:, 4992:5000]
    scale = s_ref[0]
    rows = iota((256, OB), 0)
    index = index_rows()

    def select(key, start, width, hot):
        half = (key >> 15) & 1
        mine = key & 255
        lanes = pl.ds(pl.multiple_of(start * 128, 128), width)
        z = [mm(pp_ref[p, :, lanes], hot, NN) for p in range(2)]
        return pick(rows == mine, jnp.where(half == 0, z[0], z[1]))

    def one_block(b, carry):
        key = key_ref[pl.ds(b, 1), :]
        first = jnp.minimum(kf_ref[b], NK - 2)
        _, at = obs_parts(key, first)
        spk_ref[pl.ds(b, 1), :] = select(key, first, 256, one_hot(index, at, 256)) * scale
        return carry

    lax.fori_loop(0, NB, one_block, 0, unroll=True)

    @pl.when(more > 1)
    def _():
        def one_more(b, carry):
            key = key_ref[pl.ds(b, 1), :]
            first = jnp.minimum(kf_ref[b], NK - 2)

            def window(k, t):
                _, at = obs_parts(key, k)
                return t + select(key, k, 128, one_hot(index, at, 128)) * scale

            spk_ref[pl.ds(b, 1), :] = lax.fori_loop(first + 2, kl_ref[b] + 1, window, spk_ref[pl.ds(b, 1), :])
            return carry

        lax.fori_loop(0, NB, one_more, 0)


def halves_kernel(after_hbm, a_ref, o_ref, lat_ref, lon_ref, done_ref, ap_ref):
    pad_latitude(a_ref, ap_ref)
    lat_ref[0], lat_ref[1] = split(ap_ref[...])
    lon_ref[0], lon_ref[1] = split(o_ref[...])
    done_ref[0] = 0


def observe_kernel(kf_ref, kl_ref, more_ref, key_ref, spk_ref, vb_ref, r_ref, out_ref, l_ref, part_ref):
    vh, vl = vb_ref[0], vb_ref[1]
    v1 = jnp.concatenate([vh, vl], axis=1)
    for k in range(0, NK, 2):
        h = [r_ref[:, 8 * (k + n) : 8 * (k + n) + 8, :].reshape(128, 128) for n in range(2)]
        hh, hl = split(jnp.concatenate(h, axis=1))
        field = mm(v1, jnp.concatenate([hh, hh], axis=0), NN) + mm(vh, hl, NN)
        hi, lo = split(field)
        l_ref[0:128, 128 * k : 128 * k + 256] = hi
        l_ref[128:256, 128 * k : 128 * k + 256] = lo
    rows = iota((128, OB), 0)
    index = index_rows()

    def value(row, start, width, hot):
        z = mm(l_ref[:, pl.ds(pl.multiple_of(start * 128, 128), width)], hot, NN)
        return pick(rows == row, z[0:128] + z[128:256])

    def one_block(b, carry):
        key = key_ref[pl.ds(b, 1), :]
        first = jnp.minimum(kf_ref[b], NK - 2)
        row, at = obs_parts(key, first)
        part_ref[pl.ds(b, 1), :] = value(row, first, 256, one_hot(index, at, 256))
        return carry

    lax.fori_loop(0, NB, one_block, 0, unroll=True)

    @pl.when(more_ref[0] > 1)
    def _():
        def one_more(b, carry):
            key = key_ref[pl.ds(b, 1), :]
            first = jnp.minimum(kf_ref[b], NK - 2)

            def window(k, t):
                row, at = obs_parts(key, k)
                return t + value(row, k, 128, one_hot(index, at, 128))

            part_ref[pl.ds(b, 1), :] = lax.fori_loop(first + 2, kl_ref[b] + 1, window, part_ref[pl.ds(b, 1), :])
            return carry

        lax.fori_loop(0, NB, one_more, 0)

    out_ref[...] = jnp.broadcast_to((part_ref[...] * spk_ref[...])[None], out_ref.shape)


def adjoint_kernel(kf_ref, kl_ref, more_ref, done_ref, key_ref, spk_ref, w_ref, vt_ref, ag_ref, d_ref, adj_ref, u_ref):
    adj_ref[...] = jnp.zeros_like(adj_ref)
    u_ref[...] = spk_ref[...] * (w_ref[...] * jnp.sum(ag_ref[...], axis=0))
    index = index_rows()

    def add(row, u, start, width, hot):
        mine = index[0:128] == row.astype(F32).astype(BF16)
        parts = [jnp.where(mine, x, jnp.zeros((), BF16)) for x in split(u)]
        z = mm(jnp.concatenate(parts, axis=0), hot, NT)
        adj_ref[:, pl.ds(pl.multiple_of(start * 128, 128), width)] += z[0:128] + z[128:256]

    def one_block(b, carry):
        key = key_ref[pl.ds(b, 1), :]
        first = jnp.minimum(kf_ref[b], NK - 2)
        row, at = obs_parts(key, first)
        add(row, u_ref[pl.ds(b, 1), :], first, 256, one_hot(index, at, 256))
        return carry

    lax.fori_loop(0, NB, one_block, 0, unroll=True)

    @pl.when(more_ref[0] > 1)
    def _():
        def one_more(b, carry):
            key = key_ref[pl.ds(b, 1), :]
            first = jnp.minimum(kf_ref[b], NK - 2)

            def window(k, c):
                row, at = obs_parts(key, k)
                add(row, u_ref[pl.ds(b, 1), :], k, 128, one_hot(index, at, 128))
                return c

            return lax.fori_loop(first + 2, kl_ref[b] + 1, window, carry)

        lax.fori_loop(0, NB, one_more, 0)

    th, tl = vt_ref[0], vt_ref[1]
    t1 = jnp.concatenate([th, tl], axis=1)
    for k in range(0, NK, 2):
        ah, al = split(adj_ref[:, 128 * k : 128 * k + 256])
        d = mm(t1, jnp.concatenate([ah, ah], axis=0), NN) + mm(th, al, NN)
        for n in range(2):
            d_ref[:, 8 * (k + n) : 8 * (k + n) + 8, :] = d[:, 128 * n : 128 * n + 128].reshape(16, 8, 128)


VM = pl.BlockSpec(memory_space=pltpu.VMEM)
SM = pl.BlockSpec(memory_space=pltpu.SMEM)
HB = pl.BlockSpec(memory_space=pltpu.HBM)
DMA = pltpu.SemaphoreType.DMA


def call(kernel, outs, ins, scratch, flops, nbytes, kib, name, out_specs=None):
    return pl.pallas_call(
        kernel,
        out_shape=outs,
        in_specs=ins,
        out_specs=out_specs or jax.tree.map(lambda _: VM, outs),
        scratch_shapes=scratch,
        compiler_params=pltpu.CompilerParams(vmem_limit_bytes=kib * 1024),
        cost_estimate=pl.CostEstimate(flops=flops, bytes_accessed=nbytes, transcendentals=0),
        name=name,
    )


def body(
    control,
    perturbations,
    member_scales,
    vertical_loc,
    latitude_loc,
    longitude_loc,
    observed_index,
    observed_weight,
):
    sds = jax.ShapeDtypeStruct
    rows_scratch = pltpu.VMEM((4, 8 * YS, 128), F32)
    c = control[0]
    flat = call(
        forward_kernel,
        sds((16, 160, 128), F32),
        [HB] * 3,
        [
            pltpu.VMEM((16, 160, 128), F32),
            rows_scratch,
            pltpu.VMEM((4, 200, 400), F32),
            pltpu.VMEM((200, 200), F32),
            pltpu.VMEM((400, 400), F32),
            DMA((3,)),
            DMA((4,)),
        ],
        3_000_000_000,
        4_000_000,
        64230,
        "forward",
        HB,
    )(c, latitude_loc, longitude_loc)
    columns = lax.all_to_all(flat, "lev", split_axis=0, concat_axis=0, tiled=True)

    slot = jnp.arange(2, dtype=I32)[:, None] * 128
    cell = observed_index % 5000
    key = cell * 256 + slot + observed_index // 5000
    key, weight = lax.sort((key.reshape(8192), observed_weight.reshape(8192)), num_keys=1)
    key = key.reshape(NB, OB)
    weight = weight.reshape(NB, OB)
    kf = key[:, 0] >> 16
    kl = key[:, OB - 1] >> 16
    spk, vb, vt, more = call(
        prepare_kernel,
        (
            sds((NB, OB), F32),
            sds((2, 128, 128), BF16),
            sds((2, 128, 128), BF16),
            sds((1,), I32),
        ),
        [SM, SM, SM, VM, HB, VM],
        [
            pltpu.VMEM((256, 5000), BF16),
            pltpu.VMEM((2, 256, 2560), BF16),
            DMA(()),
        ],
        4_000_000_000,
        3_000_000,
        24576,
        "prepare",
        (VM, VM, VM, SM),
    )(kf, kl, member_scales, key, perturbations.reshape(256, 5000), vertical_loc)

    copies = call(
        observe_kernel,
        sds((8, NB, OB), F32),
        [SM, SM, SM, VM, VM, VM, VM],
        [pltpu.VMEM((256, NK * 128), BF16), pltpu.VMEM((NB, OB), F32)],
        3_000_000_000,
        2_000_000,
        24576,
        "observe",
    )(kf, kl, more, key, spk, vb, columns)
    gathered = lax.all_to_all(copies, "mem", split_axis=0, concat_axis=0, tiled=True)
    lat, lon, done = call(
        halves_kernel,
        (sds((2, 256, 200), BF16), sds((2, 400, 400), BF16), sds((1,), I32)),
        [HB, VM, VM],
        [pltpu.VMEM((256, 200), F32)],
        1_000_000,
        2_000_000,
        24576,
        "halves",
        (VM, VM, SM),
    )(copies, latitude_loc, longitude_loc)
    adjoint = call(
        adjoint_kernel,
        sds((16, 160, 128), F32),
        [SM, SM, SM, SM, VM, VM, VM, VM, VM],
        [pltpu.VMEM((128, NK * 128), F32), pltpu.VMEM((NB, OB), F32)],
        3_000_000_000,
        2_000_000,
        24576,
        "adjoint",
    )(kf, kl, more, done, key, spk, weight, vt, gathered)
    levels = lax.all_to_all(adjoint, "lev", split_axis=0, concat_axis=0, tiled=True)
    result = call(
        backward_kernel,
        sds((4, 200, 400), F32),
        [VM] * 4,
        [rows_scratch, pltpu.VMEM((4, 200, 400), F32), DMA((4,))],
        3_000_000_000,
        5_000_000,
        24576,
        "backward",
        HB,
    )(levels, c, lat, lon)
    return result[None]


def solution(mesh):
    placed = (
        P("mem", "lev", None, None),
        P("mem", None, None, None, "lev"),
        P("mem"),
        P(),
        P(),
        P(),
        P(None, "lev"),
        P(None, "lev"),
    )
    return jax.shard_map(
        body, mesh=mesh, in_specs=placed, out_specs=P("mem", "lev", None, None), check_vma=False
    )
```

```python
import functools

import jax
import jax.numpy as jnp
from jax import lax
from jax.experimental import pallas as pl
from jax.experimental.pallas import tpu as pltpu
from jax.sharding import PartitionSpec as P

F32 = jnp.float32
BF16 = jnp.bfloat16
I32 = jnp.int32

NB = 32
OB = 256
NK = 20
YS = 136
NN = (((1,), (0,)), ((), ()))
NT = (((1,), (1,)), ((), ()))
TN = (((0,), (0,)), ((), ()))


def split(x):
    hi = x.astype(BF16)
    return hi, (x - hi.astype(F32)).astype(BF16)


def mm(a, b, dims):
    return lax.dot_general(a, b, dims, preferred_element_type=F32)


def mm3(a, b, dims=NN):
    return mm(a[0], b[0], dims) + (mm(a[0], b[1], dims) + mm(a[1], b[0], dims))


def pad_latitude(a_ref, ap_ref):
    ap_ref[...] = jnp.zeros_like(ap_ref)
    for i in range(8):
        row = (i % 2) * 128 + (i // 2) * 32
        ap_ref[row : row + 25, :] = a_ref[25 * i : 25 * i + 25, :]


def iota(shape, dim):
    return lax.broadcasted_iota(I32, shape, dim)


def forward_kernel(c_hbm, a_hbm, o_hbm, f_hbm, f_ref, y_ref, q_ref, c_ref, a_ref, o_ref, sem, out_sem):
    reads = [
        pltpu.make_async_copy(a_hbm, a_ref, sem.at[0]),
        pltpu.make_async_copy(c_hbm, c_ref, sem.at[1]),
        pltpu.make_async_copy(o_hbm, o_ref, sem.at[2]),
    ]
    for copy in reads:
        copy.start()
    reads[0].wait()
    reads[1].wait()
    lat = split(a_ref[...])
    for l in range(4):
        q_ref[200 * l : 200 * l + 200, :] = mm3(lat, split(c_ref[l]))
    reads[2].wait()
    lon = split(o_ref[...])
    field = mm3(split(q_ref[...]), lon, NT)
    for l in range(4):
        for i in range(8):
            row = (4 * (i % 2) + l) * YS + 32 * (i // 2)
            part = field[200 * l + 25 * i : 200 * l + 25 * i + 25]
            for j in range(3):
                y_ref[j, row : row + 25, :] = part[:, 128 * j : 128 * j + 128]
            y_ref[3, row : row + 25, 0:16] = part[:, 384:400]

    lane = iota((8, 128), 1)
    upper = iota((8, 128), 0) < 4

    def write(w):
        blocks = pl.ds(4 * w, 4)
        return pltpu.make_async_copy(f_ref.at[blocks], f_hbm.at[blocks], out_sem.at[w])

    def one_w(w, carry):
        loaded = {}

        def load(r, j):
            if (r, j) not in loaded:
                loaded[(r, j)] = y_ref[j, pl.ds(w * 32 + r, 8, stride=YS), :]
            return loaded[(r, j)]

        def chunk(e, i):
            first = 5000 * e + 128 * i
            count = min(128, 5000 - 128 * i)
            done = 0
            value = None
            while done < count:
                r, o = divmod(first + done, 400)
                j, s = divmod(o, 128)
                n = min(128 - s, 400 - o, count - done)
                shift = (done - s) % 128
                piece = load(r, j)
                if shift:
                    piece = pltpu.roll(piece, shift, 1)
                value = piece if value is None else jnp.where(lane < done, value, piece)
                done += n
            if count < 128:
                value = jnp.where(lane < count, value, 0.0)
            return value

        for e in range(2):
            for k in range(NK):
                x0 = chunk(e, 2 * k)
                x1 = chunk(e, 2 * k + 1)
                f_ref[4 * w + e, 8 * k : 8 * k + 8, :] = jnp.where(upper, x0, pltpu.roll(x1, 4, 0))
                f_ref[4 * w + 2 + e, 8 * k : 8 * k + 8, :] = jnp.where(upper, pltpu.roll(x0, 4, 0), x1)
        write(w).start()
        return carry

    lax.fori_loop(0, 4, one_w, 0)
    for w in range(4):
        write(w).wait()


def backward_kernel(d_ref, c_ref, lat_ref, lon_ref, h_hbm, y_ref, q_ref, h_ref, sem):
    for j in range(4):
        for g in range(8):
            for w in range(4):
                row = g * YS + w * 32 + 25
                y_ref[j, row : row + 7, :] = jnp.zeros((7, 128), F32)
    lane = iota((8, 128), 1)
    upper = iota((8, 128), 0) < 4

    def one_w(w, carry):
        chunks = {}

        def chunk(e, i):
            if (e, i) not in chunks:
                k = i // 2
                t0 = d_ref[4 * w + e, 8 * k : 8 * k + 8, :]
                t1 = d_ref[4 * w + 2 + e, 8 * k : 8 * k + 8, :]
                chunks[(e, 2 * k)] = jnp.where(upper, t0, pltpu.roll(t1, 4, 0))
                chunks[(e, 2 * k + 1)] = jnp.where(upper, pltpu.roll(t0, 4, 0), t1)
            return chunks[(e, i)]

        for r in range(25):
            for j in range(4):
                first = 400 * r + 128 * j
                count = min(128, 400 - 128 * j)
                done = 0
                value = None
                while done < count:
                    e, c = divmod(first + done, 5000)
                    i, s = divmod(c, 128)
                    n = min(128 - s, 5000 - c, count - done)
                    shift = (done - s) % 128
                    piece = chunk(e, i)
                    if shift:
                        piece = pltpu.roll(piece, shift, 1)
                    value = piece if value is None else jnp.where(lane < done, value, piece)
                    done += n
                y_ref[j, pl.ds(w * 32 + r, 8, stride=YS), :] = value
        return carry

    lax.fori_loop(0, 4, one_w, 0)
    writes = []
    lat = (lat_ref[0], lat_ref[1])
    lon = (lon_ref[0], lon_ref[1])
    for l in range(4):
        field = jnp.concatenate(
            [
                jnp.concatenate([y_ref[j, (4 * u + l) * YS : (4 * u + l) * YS + 128, :] for j in range(4)], axis=1)
                for u in range(2)
            ],
            axis=0,
        )
        q_ref[200 * l : 200 * l + 200, :] = mm3(lat, split(field), TN)[:, :400]
    for l in range(4):
        if l % 2 == 0:
            pair = mm3(split(q_ref[200 * l : 200 * l + 400, :]), lon)
        h_ref[l] = c_ref[l] + pair[200 * (l % 2) : 200 * (l % 2) + 200]
        writes.append(pltpu.make_async_copy(h_ref.at[l], h_hbm.at[l], sem.at[l]))
        writes[l].start()
    for copy in writes:
        copy.wait()


def obs_parts(key, first):
    cell = (key >> 8) - first * 256
    row = ((cell >> 7) & 1) * 64 + (key & 63)
    return row, (cell >> 8) * 128 + (cell & 127)


def index_rows():
    return iota((256, OB), 0).astype(F32).astype(BF16)


def one_hot(index, at, width):
    return jnp.where(index[0:width] == at.astype(F32).astype(BF16), jnp.ones((), BF16), jnp.zeros((), BF16))


def pick(mask, z):
    return jnp.sum(jnp.where(mask, z, 0.0), axis=0, keepdims=True)


def prepare_kernel(
    n_ref, s_ref, key_ref, p_hbm, v_ref, spk_ref, vb_ref, vt_ref, p_ref, pp_ref, sem
):
    copy = pltpu.make_async_copy(p_hbm, p_ref, sem)
    copy.start()
    take = [
        (((iota((64, 128), 1) // 8) * 4 + iota((64, 128), 1) % 4 == iota((64, 128), 0)) & ((iota((64, 128), 1) // 4) % 2 == p))
        .astype(F32)
        .astype(BF16)
        for p in range(2)
    ]
    put = [(iota((128, 64), 0) == iota((128, 64), 1) + 64 * p).astype(F32).astype(BF16) for p in range(2)]
    for n, v in enumerate(split(v_ref[...])):
        big = jnp.zeros((128, 128), F32)
        for p in range(2):
            wide = mm(v, take[p], NN).astype(BF16)
            big = big + mm(put[p], wide, NN)
        vb_ref[n] = big.astype(BF16)
        vt_ref[n] = big.T.astype(BF16)

    copy.wait()
    for i in range(2 * NK - 1):
        pp_ref[i % 2, :, 128 * (i // 2) : 128 * (i // 2) + 128] = p_ref[:, 128 * i : 128 * i + 128]
    pp_ref[1, :, 2432:2560] = jnp.zeros((256, 128), BF16)
    pp_ref[1, :, 2432:2440] = p_ref[:, 4992:5000]
    scale = s_ref[0]
    rows = iota((256, OB), 0)
    index = index_rows()

    def select(key, start, width, hot):
        half = (key >> 15) & 1
        mine = key & 255
        lanes = pl.ds(pl.multiple_of(start * 128, 128), width)
        z = [mm(pp_ref[p, :, lanes], hot, NN) for p in range(2)]
        return pick(rows == mine, jnp.where(half == 0, z[0], z[1]))

    def one_block(b, carry):
        key = key_ref[pl.ds(b, 1), :]
        first = jnp.minimum(n_ref[b], NK - 2)
        _, at = obs_parts(key, first)
        spk_ref[pl.ds(b, 1), :] = select(key, first, 256, one_hot(index, at, 256)) * scale
        return carry

    lax.fori_loop(0, NB, one_block, 0, unroll=True)

    @pl.when(n_ref[2 * NB] > 1)
    def _():
        def one_more(b, carry):
            key = key_ref[pl.ds(b, 1), :]
            first = jnp.minimum(n_ref[b], NK - 2)

            def window(k, t):
                _, at = obs_parts(key, k)
                return t + select(key, k, 128, one_hot(index, at, 128)) * scale

            spk_ref[pl.ds(b, 1), :] = lax.fori_loop(first + 2, n_ref[NB + b] + 1, window, spk_ref[pl.ds(b, 1), :])
            return carry

        lax.fori_loop(0, NB, one_more, 0)


def halves_kernel(after_hbm, a_ref, o_ref, lat_ref, lon_ref, ap_ref):
    pad_latitude(a_ref, ap_ref)
    lat_ref[0], lat_ref[1] = split(ap_ref[...])
    lon_ref[0], lon_ref[1] = split(o_ref[...])


def observe_kernel(n_ref, key_ref, spk_ref, vb_ref, r_ref, out_ref, l_ref, part_ref):
    vh, vl = vb_ref[0], vb_ref[1]
    v1 = jnp.concatenate([vh, vl], axis=1)
    for k in range(0, NK, 2):
        h = [r_ref[:, 8 * (k + n) : 8 * (k + n) + 8, :].reshape(128, 128) for n in range(2)]
        hh, hl = split(jnp.concatenate(h, axis=1))
        field = mm(v1, jnp.concatenate([hh, hh], axis=0), NN) + mm(vh, hl, NN)
        hi, lo = split(field)
        l_ref[0:128, 128 * k : 128 * k + 256] = hi
        l_ref[128:256, 128 * k : 128 * k + 256] = lo
    rows = iota((128, OB), 0)
    index = index_rows()

    def value(row, start, width, hot):
        z = mm(l_ref[:, pl.ds(pl.multiple_of(start * 128, 128), width)], hot, NN)
        return pick(rows == row, z[0:128] + z[128:256])

    def one_block(b, carry):
        key = key_ref[pl.ds(b, 1), :]
        first = jnp.minimum(n_ref[b], NK - 2)
        row, at = obs_parts(key, first)
        part_ref[pl.ds(b, 1), :] = value(row, first, 256, one_hot(index, at, 256))
        return carry

    lax.fori_loop(0, NB, one_block, 0, unroll=True)

    @pl.when(n_ref[2 * NB] > 1)
    def _():
        def one_more(b, carry):
            key = key_ref[pl.ds(b, 1), :]
            first = jnp.minimum(n_ref[b], NK - 2)

            def window(k, t):
                row, at = obs_parts(key, k)
                return t + value(row, k, 128, one_hot(index, at, 128))

            part_ref[pl.ds(b, 1), :] = lax.fori_loop(first + 2, n_ref[NB + b] + 1, window, part_ref[pl.ds(b, 1), :])
            return carry

        lax.fori_loop(0, NB, one_more, 0)

    out_ref[...] = jnp.broadcast_to((part_ref[...] * spk_ref[...])[None], out_ref.shape)


def adjoint_kernel(n_ref, after_hbm, key_ref, spk_ref, w_ref, vt_ref, ag_ref, d_ref, adj_ref, u_ref):
    adj_ref[...] = jnp.zeros_like(adj_ref)
    u_ref[...] = spk_ref[...] * (w_ref[...] * jnp.sum(ag_ref[...], axis=0))
    index = index_rows()

    def add(row, u, start, width, hot):
        mine = index[0:128] == row.astype(F32).astype(BF16)
        parts = [jnp.where(mine, x, jnp.zeros((), BF16)) for x in split(u)]
        z = mm(jnp.concatenate(parts, axis=0), hot, NT)
        adj_ref[:, pl.ds(pl.multiple_of(start * 128, 128), width)] += z[0:128] + z[128:256]

    def one_block(b, carry):
        key = key_ref[pl.ds(b, 1), :]
        first = jnp.minimum(n_ref[b], NK - 2)
        row, at = obs_parts(key, first)
        add(row, u_ref[pl.ds(b, 1), :], first, 256, one_hot(index, at, 256))
        return carry

    lax.fori_loop(0, NB, one_block, 0, unroll=True)

    @pl.when(n_ref[2 * NB] > 1)
    def _():
        def one_more(b, carry):
            key = key_ref[pl.ds(b, 1), :]
            first = jnp.minimum(n_ref[b], NK - 2)

            def window(k, c):
                row, at = obs_parts(key, k)
                add(row, u_ref[pl.ds(b, 1), :], k, 128, one_hot(index, at, 128))
                return c

            return lax.fori_loop(first + 2, n_ref[NB + b] + 1, window, carry)

        lax.fori_loop(0, NB, one_more, 0)

    th, tl = vt_ref[0], vt_ref[1]
    t1 = jnp.concatenate([th, tl], axis=1)
    for k in range(0, NK, 2):
        ah, al = split(adj_ref[:, 128 * k : 128 * k + 256])
        d = mm(t1, jnp.concatenate([ah, ah], axis=0), NN) + mm(th, al, NN)
        for n in range(2):
            d_ref[:, 8 * (k + n) : 8 * (k + n) + 8, :] = d[:, 128 * n : 128 * n + 128].reshape(16, 8, 128)


VM = pl.BlockSpec(memory_space=pltpu.VMEM)
SM = pl.BlockSpec(memory_space=pltpu.SMEM)
HB = pl.BlockSpec(memory_space=pltpu.HBM)
DMA = pltpu.SemaphoreType.DMA


def call(kernel, outs, ins, scratch, flops, nbytes, kib, name, out_specs=None):
    return pl.pallas_call(
        kernel,
        out_shape=outs,
        in_specs=ins,
        out_specs=out_specs or jax.tree.map(lambda _: VM, outs),
        scratch_shapes=scratch,
        compiler_params=pltpu.CompilerParams(vmem_limit_bytes=kib * 1024),
        cost_estimate=pl.CostEstimate(flops=flops, bytes_accessed=nbytes, transcendentals=0),
        name=name,
    )


def body(
    control,
    perturbations,
    member_scales,
    vertical_loc,
    latitude_loc,
    longitude_loc,
    observed_index,
    observed_weight,
):
    sds = jax.ShapeDtypeStruct
    rows_scratch = pltpu.VMEM((4, 8 * YS, 128), F32)
    c = control[0]
    flat = call(
        forward_kernel,
        sds((16, 160, 128), F32),
        [HB] * 3,
        [
            pltpu.VMEM((16, 160, 128), F32),
            rows_scratch,
            pltpu.VMEM((800, 400), F32),
            pltpu.VMEM((4, 200, 400), F32),
            pltpu.VMEM((200, 200), F32),
            pltpu.VMEM((400, 400), F32),
            DMA((3,)),
            DMA((4,)),
        ],
        3_000_000_000,
        4_000_000,
        64230,
        "forward",
        HB,
    )(c, latitude_loc, longitude_loc)
    columns = lax.all_to_all(flat, "lev", split_axis=0, concat_axis=0, tiled=True)

    slot = jnp.arange(2, dtype=I32)[:, None] * 128
    cell = observed_index % 5000
    key = cell * 256 + slot + observed_index // 5000
    key, weight = lax.sort((key.reshape(8192), observed_weight.reshape(8192)), num_keys=1)
    key = key.reshape(NB, OB)
    weight = weight.reshape(NB, OB)
    kf = key[:, 0] >> 16
    kl = key[:, OB - 1] >> 16
    spans = jnp.concatenate([kf, kl, jnp.max(kl - jnp.minimum(kf, NK - 2), keepdims=True)])
    spk, vb, vt = call(
        prepare_kernel,
        (
            sds((NB, OB), F32),
            sds((2, 128, 128), BF16),
            sds((2, 128, 128), BF16),
        ),
        [SM, SM, VM, HB, VM],
        [
            pltpu.VMEM((256, 5000), BF16),
            pltpu.VMEM((2, 256, 2560), BF16),
            DMA(()),
        ],
        4_000_000_000,
        3_000_000,
        24576,
        "prepare",
    )(spans, member_scales, key, perturbations.reshape(256, 5000), vertical_loc)

    copies = call(
        observe_kernel,
        sds((8, NB, OB), F32),
        [SM, VM, VM, VM, VM],
        [pltpu.VMEM((256, NK * 128), BF16), pltpu.VMEM((NB, OB), F32)],
        3_000_000_000,
        2_000_000,
        24576,
        "observe",
    )(spans, key, spk, vb, columns)
    gathered = lax.all_to_all(copies, "mem", split_axis=0, concat_axis=0, tiled=True)
    lat, lon = call(
        halves_kernel,
        (sds((2, 256, 200), BF16), sds((2, 400, 400), BF16)),
        [HB, VM, VM],
        [pltpu.VMEM((256, 200), F32)],
        1_000_000,
        2_000_000,
        24576,
        "halves",
    )(copies, latitude_loc, longitude_loc)
    adjoint = call(
        adjoint_kernel,
        sds((16, 160, 128), F32),
        [SM, HB, VM, VM, VM, VM, VM],
        [pltpu.VMEM((128, NK * 128), F32), pltpu.VMEM((NB, OB), F32)],
        3_000_000_000,
        2_000_000,
        24576,
        "adjoint",
    )(spans, lat, key, spk, weight, vt, gathered)
    levels = lax.all_to_all(adjoint, "lev", split_axis=0, concat_axis=0, tiled=True)
    result = call(
        backward_kernel,
        sds((4, 200, 400), F32),
        [VM] * 4,
        [rows_scratch, pltpu.VMEM((800, 400), F32), pltpu.VMEM((4, 200, 400), F32), DMA((4,))],
        3_000_000_000,
        5_000_000,
        24576,
        "backward",
        HB,
    )(levels, c, lat, lon)
    return result[None]


def solution(mesh):
    placed = (
        P("mem", "lev", None, None),
        P("mem", None, None, None, "lev"),
        P("mem"),
        P(),
        P(),
        P(),
        P(None, "lev"),
        P(None, "lev"),
    )
    return jax.shard_map(
        body, mesh=mesh, in_specs=placed, out_specs=P("mem", "lev", None, None), check_vma=False
    )
```

```python
import functools

import jax
import jax.numpy as jnp
from jax import lax
from jax.experimental import pallas as pl
from jax.experimental.pallas import tpu as pltpu
from jax.sharding import PartitionSpec as P

F32 = jnp.float32
BF16 = jnp.bfloat16
I32 = jnp.int32

NB = 32
OB = 256
NK = 20
YS = 136
NN = (((1,), (0,)), ((), ()))
NT = (((1,), (1,)), ((), ()))
TN = (((0,), (0,)), ((), ()))


def split(x):
    hi = x.astype(BF16)
    return hi, (x - hi.astype(F32)).astype(BF16)


def mm(a, b, dims):
    return lax.dot_general(a, b, dims, preferred_element_type=F32)


def mm3(a, b, dims=NN):
    return mm(a[0], b[0], dims) + (mm(a[0], b[1], dims) + mm(a[1], b[0], dims))


def pad_latitude(a_ref, ap_ref):
    ap_ref[...] = jnp.zeros_like(ap_ref)
    for i in range(8):
        row = (i % 2) * 128 + (i // 2) * 32
        ap_ref[row : row + 25, :] = a_ref[25 * i : 25 * i + 25, :]


def iota(shape, dim):
    return lax.broadcasted_iota(I32, shape, dim)


def forward_kernel(c_hbm, a_hbm, o_hbm, f_hbm, f_ref, y_ref, q_ref, c_ref, a_ref, o_ref, sem, out_sem):
    reads = [
        pltpu.make_async_copy(a_hbm, a_ref, sem.at[0]),
        pltpu.make_async_copy(c_hbm, c_ref, sem.at[1]),
        pltpu.make_async_copy(o_hbm, o_ref, sem.at[2]),
    ]
    for copy in reads:
        copy.start()
    reads[0].wait()
    reads[1].wait()
    lat = split(a_ref[...])
    for l in range(4):
        q_ref[200 * l : 200 * l + 200, :] = mm3(lat, split(c_ref[l]))
    reads[2].wait()
    lon = split(o_ref[...])
    field = mm3(split(q_ref[...]), lon, NT)
    for l in range(4):
        for i in range(8):
            row = (4 * (i % 2) + l) * YS + 32 * (i // 2)
            part = field[200 * l + 25 * i : 200 * l + 25 * i + 25]
            for j in range(3):
                y_ref[j, row : row + 25, :] = part[:, 128 * j : 128 * j + 128]
            y_ref[3, row : row + 25, 0:16] = part[:, 384:400]

    lane = iota((8, 128), 1)
    upper = iota((8, 128), 0) < 4

    def write(w):
        blocks = pl.ds(4 * w, 4)
        return pltpu.make_async_copy(f_ref.at[blocks], f_hbm.at[blocks], out_sem.at[w])

    def one_w(w, carry):
        loaded = {}

        def load(r, j):
            if (r, j) not in loaded:
                loaded[(r, j)] = y_ref[j, pl.ds(w * 32 + r, 8, stride=YS), :]
            return loaded[(r, j)]

        def chunk(e, i):
            first = 5000 * e + 128 * i
            count = min(128, 5000 - 128 * i)
            done = 0
            value = None
            while done < count:
                r, o = divmod(first + done, 400)
                j, s = divmod(o, 128)
                n = min(128 - s, 400 - o, count - done)
                shift = (done - s) % 128
                piece = load(r, j)
                if shift:
                    piece = pltpu.roll(piece, shift, 1)
                value = piece if value is None else jnp.where(lane < done, value, piece)
                done += n
            if count < 128:
                value = jnp.where(lane < count, value, 0.0)
            return value

        for e in range(2):
            for k in range(NK):
                x0 = chunk(e, 2 * k)
                x1 = chunk(e, 2 * k + 1)
                f_ref[4 * w + e, 8 * k : 8 * k + 8, :] = jnp.where(upper, x0, pltpu.roll(x1, 4, 0))
                f_ref[4 * w + 2 + e, 8 * k : 8 * k + 8, :] = jnp.where(upper, pltpu.roll(x0, 4, 0), x1)
        write(w).start()
        return carry

    lax.fori_loop(0, 4, one_w, 0, unroll=True)
    for w in range(4):
        write(w).wait()


def backward_kernel(d_ref, c_ref, lat_ref, lon_ref, h_hbm, y_ref, q_ref, h_ref, sem):
    for j in range(4):
        for g in range(8):
            for w in range(4):
                row = g * YS + w * 32 + 25
                y_ref[j, row : row + 7, :] = jnp.zeros((7, 128), F32)
    lane = iota((8, 128), 1)
    upper = iota((8, 128), 0) < 4

    def one_w(w, carry):
        chunks = {}

        def chunk(e, i):
            if (e, i) not in chunks:
                k = i // 2
                t0 = d_ref[4 * w + e, 8 * k : 8 * k + 8, :]
                t1 = d_ref[4 * w + 2 + e, 8 * k : 8 * k + 8, :]
                chunks[(e, 2 * k)] = jnp.where(upper, t0, pltpu.roll(t1, 4, 0))
                chunks[(e, 2 * k + 1)] = jnp.where(upper, pltpu.roll(t0, 4, 0), t1)
            return chunks[(e, i)]

        for r in range(25):
            for j in range(4):
                first = 400 * r + 128 * j
                count = min(128, 400 - 128 * j)
                done = 0
                value = None
                while done < count:
                    e, c = divmod(first + done, 5000)
                    i, s = divmod(c, 128)
                    n = min(128 - s, 5000 - c, count - done)
                    shift = (done - s) % 128
                    piece = chunk(e, i)
                    if shift:
                        piece = pltpu.roll(piece, shift, 1)
                    value = piece if value is None else jnp.where(lane < done, value, piece)
                    done += n
                y_ref[j, pl.ds(w * 32 + r, 8, stride=YS), :] = value
        return carry

    lax.fori_loop(0, 4, one_w, 0, unroll=True)
    writes = []
    lat = (lat_ref[0], lat_ref[1])
    lon = (lon_ref[0], lon_ref[1])
    for l in range(4):
        field = jnp.concatenate(
            [
                jnp.concatenate([y_ref[j, (4 * u + l) * YS : (4 * u + l) * YS + 128, :] for j in range(4)], axis=1)
                for u in range(2)
            ],
            axis=0,
        )
        q_ref[200 * l : 200 * l + 200, :] = mm3(lat, split(field), TN)[:, :400]
    for l in range(4):
        if l % 2 == 0:
            pair = mm3(split(q_ref[200 * l : 200 * l + 400, :]), lon)
        h_ref[l] = c_ref[l] + pair[200 * (l % 2) : 200 * (l % 2) + 200]
        writes.append(pltpu.make_async_copy(h_ref.at[l], h_hbm.at[l], sem.at[l]))
        writes[l].start()
    for copy in writes:
        copy.wait()


def obs_parts(key, first):
    cell = (key >> 8) - first * 256
    row = ((cell >> 7) & 1) * 64 + (key & 63)
    return row, (cell >> 8) * 128 + (cell & 127)


def index_rows():
    return iota((256, OB), 0).astype(F32).astype(BF16)


def one_hot(index, at, width):
    return jnp.where(index[0:width] == at.astype(F32).astype(BF16), jnp.ones((), BF16), jnp.zeros((), BF16))


def pick(mask, z):
    return jnp.sum(jnp.where(mask, z, 0.0), axis=0, keepdims=True)


def prepare_kernel(
    n_ref, s_ref, key_ref, p_hbm, v_ref, spk_ref, vb_ref, vt_ref, p_ref, pp_ref, sem
):
    copy = pltpu.make_async_copy(p_hbm, p_ref, sem)
    copy.start()
    take = [
        (((iota((64, 128), 1) // 8) * 4 + iota((64, 128), 1) % 4 == iota((64, 128), 0)) & ((iota((64, 128), 1) // 4) % 2 == p))
        .astype(F32)
        .astype(BF16)
        for p in range(2)
    ]
    put = [(iota((128, 64), 0) == iota((128, 64), 1) + 64 * p).astype(F32).astype(BF16) for p in range(2)]
    for n, v in enumerate(split(v_ref[...])):
        big = jnp.zeros((128, 128), F32)
        for p in range(2):
            wide = mm(v, take[p], NN).astype(BF16)
            big = big + mm(put[p], wide, NN)
        vb_ref[n] = big.astype(BF16)
        vt_ref[n] = big.T.astype(BF16)

    copy.wait()
    for i in range(2 * NK - 1):
        pp_ref[i % 2, :, 128 * (i // 2) : 128 * (i // 2) + 128] = p_ref[:, 128 * i : 128 * i + 128]
    pp_ref[1, :, 2432:2560] = jnp.zeros((256, 128), BF16)
    pp_ref[1, :, 2432:2440] = p_ref[:, 4992:5000]
    scale = s_ref[0]
    rows = iota((256, OB), 0)
    index = index_rows()

    def select(key, start, width, hot):
        half = (key >> 15) & 1
        mine = key & 255
        lanes = pl.ds(pl.multiple_of(start * 128, 128), width)
        z = [mm(pp_ref[p, :, lanes], hot, NN) for p in range(2)]
        return pick(rows == mine, jnp.where(half == 0, z[0], z[1]))

    def one_block(b, carry):
        key = key_ref[pl.ds(b, 1), :]
        first = jnp.minimum(n_ref[b], NK - 2)
        _, at = obs_parts(key, first)
        spk_ref[pl.ds(b, 1), :] = select(key, first, 256, one_hot(index, at, 256)) * scale
        return carry

    lax.fori_loop(0, NB, one_block, 0, unroll=True)

    @pl.when(n_ref[2 * NB] > 1)
    def _():
        def one_more(b, carry):
            key = key_ref[pl.ds(b, 1), :]
            first = jnp.minimum(n_ref[b], NK - 2)

            def window(k, t):
                _, at = obs_parts(key, k)
                return t + select(key, k, 128, one_hot(index, at, 128)) * scale

            spk_ref[pl.ds(b, 1), :] = lax.fori_loop(first + 2, n_ref[NB + b] + 1, window, spk_ref[pl.ds(b, 1), :])
            return carry

        lax.fori_loop(0, NB, one_more, 0)


def halves_kernel(after_hbm, a_ref, o_ref, lat_ref, lon_ref, ap_ref):
    pad_latitude(a_ref, ap_ref)
    lat_ref[0], lat_ref[1] = split(ap_ref[...])
    lon_ref[0], lon_ref[1] = split(o_ref[...])


def observe_kernel(n_ref, key_ref, spk_ref, vb_ref, r_ref, out_ref, l_ref, part_ref):
    vh, vl = vb_ref[0], vb_ref[1]
    v1 = jnp.concatenate([vh, vl], axis=1)
    for k in range(0, NK, 2):
        h = [r_ref[:, 8 * (k + n) : 8 * (k + n) + 8, :].reshape(128, 128) for n in range(2)]
        hh, hl = split(jnp.concatenate(h, axis=1))
        field = mm(v1, jnp.concatenate([hh, hh], axis=0), NN) + mm(vh, hl, NN)
        hi, lo = split(field)
        l_ref[0:128, 128 * k : 128 * k + 256] = hi
        l_ref[128:256, 128 * k : 128 * k + 256] = lo
    rows = iota((128, OB), 0)
    index = index_rows()

    def value(row, start, width, hot):
        z = mm(l_ref[:, pl.ds(pl.multiple_of(start * 128, 128), width)], hot, NN)
        return pick(rows == row, z[0:128] + z[128:256])

    def one_block(b, carry):
        key = key_ref[pl.ds(b, 1), :]
        first = jnp.minimum(n_ref[b], NK - 2)
        row, at = obs_parts(key, first)
        part_ref[pl.ds(b, 1), :] = value(row, first, 256, one_hot(index, at, 256))
        return carry

    lax.fori_loop(0, NB, one_block, 0, unroll=True)

    @pl.when(n_ref[2 * NB] > 1)
    def _():
        def one_more(b, carry):
            key = key_ref[pl.ds(b, 1), :]
            first = jnp.minimum(n_ref[b], NK - 2)

            def window(k, t):
                row, at = obs_parts(key, k)
                return t + value(row, k, 128, one_hot(index, at, 128))

            part_ref[pl.ds(b, 1), :] = lax.fori_loop(first + 2, n_ref[NB + b] + 1, window, part_ref[pl.ds(b, 1), :])
            return carry

        lax.fori_loop(0, NB, one_more, 0)

    out_ref[...] = jnp.broadcast_to((part_ref[...] * spk_ref[...])[None], out_ref.shape)


def adjoint_kernel(n_ref, after_hbm, key_ref, spk_ref, w_ref, vt_ref, ag_ref, d_ref, adj_ref, u_ref):
    adj_ref[...] = jnp.zeros_like(adj_ref)
    u_ref[...] = spk_ref[...] * (w_ref[...] * jnp.sum(ag_ref[...], axis=0))
    index = index_rows()

    def add(row, u, start, width, hot):
        mine = index[0:128] == row.astype(F32).astype(BF16)
        parts = [jnp.where(mine, x, jnp.zeros((), BF16)) for x in split(u)]
        z = mm(jnp.concatenate(parts, axis=0), hot, NT)
        adj_ref[:, pl.ds(pl.multiple_of(start * 128, 128), width)] += z[0:128] + z[128:256]

    def one_block(b, carry):
        key = key_ref[pl.ds(b, 1), :]
        first = jnp.minimum(n_ref[b], NK - 2)
        row, at = obs_parts(key, first)
        add(row, u_ref[pl.ds(b, 1), :], first, 256, one_hot(index, at, 256))
        return carry

    lax.fori_loop(0, NB, one_block, 0, unroll=True)

    @pl.when(n_ref[2 * NB] > 1)
    def _():
        def one_more(b, carry):
            key = key_ref[pl.ds(b, 1), :]
            first = jnp.minimum(n_ref[b], NK - 2)

            def window(k, c):
                row, at = obs_parts(key, k)
                add(row, u_ref[pl.ds(b, 1), :], k, 128, one_hot(index, at, 128))
                return c

            return lax.fori_loop(first + 2, n_ref[NB + b] + 1, window, carry)

        lax.fori_loop(0, NB, one_more, 0)

    th, tl = vt_ref[0], vt_ref[1]
    t1 = jnp.concatenate([th, tl], axis=1)
    for k in range(0, NK, 2):
        ah, al = split(adj_ref[:, 128 * k : 128 * k + 256])
        d = mm(t1, jnp.concatenate([ah, ah], axis=0), NN) + mm(th, al, NN)
        for n in range(2):
            d_ref[:, 8 * (k + n) : 8 * (k + n) + 8, :] = d[:, 128 * n : 128 * n + 128].reshape(16, 8, 128)


VM = pl.BlockSpec(memory_space=pltpu.VMEM)
SM = pl.BlockSpec(memory_space=pltpu.SMEM)
HB = pl.BlockSpec(memory_space=pltpu.HBM)
DMA = pltpu.SemaphoreType.DMA


def call(kernel, outs, ins, scratch, flops, nbytes, kib, name, out_specs=None):
    return pl.pallas_call(
        kernel,
        out_shape=outs,
        in_specs=ins,
        out_specs=out_specs or jax.tree.map(lambda _: VM, outs),
        scratch_shapes=scratch,
        compiler_params=pltpu.CompilerParams(vmem_limit_bytes=kib * 1024),
        cost_estimate=pl.CostEstimate(flops=flops, bytes_accessed=nbytes, transcendentals=0),
        name=name,
    )


def body(
    control,
    perturbations,
    member_scales,
    vertical_loc,
    latitude_loc,
    longitude_loc,
    observed_index,
    observed_weight,
):
    sds = jax.ShapeDtypeStruct
    rows_scratch = pltpu.VMEM((4, 8 * YS, 128), F32)
    c = control[0]
    flat = call(
        forward_kernel,
        sds((16, 160, 128), F32),
        [HB] * 3,
        [
            pltpu.VMEM((16, 160, 128), F32),
            rows_scratch,
            pltpu.VMEM((800, 400), F32),
            pltpu.VMEM((4, 200, 400), F32),
            pltpu.VMEM((200, 200), F32),
            pltpu.VMEM((400, 400), F32),
            DMA((3,)),
            DMA((4,)),
        ],
        3_000_000_000,
        4_000_000,
        64230,
        "forward",
        HB,
    )(c, latitude_loc, longitude_loc)
    columns = lax.all_to_all(flat, "lev", split_axis=0, concat_axis=0, tiled=True)

    slot = jnp.arange(2, dtype=I32)[:, None] * 128
    cell = observed_index % 5000
    key = cell * 256 + slot + observed_index // 5000
    key, weight = lax.sort((key.reshape(8192), observed_weight.reshape(8192)), num_keys=1)
    key = key.reshape(NB, OB)
    weight = weight.reshape(NB, OB)
    kf = key[:, 0] >> 16
    kl = key[:, OB - 1] >> 16
    spans = jnp.concatenate([kf, kl, jnp.max(kl - jnp.minimum(kf, NK - 2), keepdims=True)])
    spk, vb, vt = call(
        prepare_kernel,
        (
            sds((NB, OB), F32),
            sds((2, 128, 128), BF16),
            sds((2, 128, 128), BF16),
        ),
        [SM, SM, VM, HB, VM],
        [
            pltpu.VMEM((256, 5000), BF16),
            pltpu.VMEM((2, 256, 2560), BF16),
            DMA(()),
        ],
        4_000_000_000,
        3_000_000,
        24576,
        "prepare",
    )(spans, member_scales, key, perturbations.reshape(256, 5000), vertical_loc)

    copies = call(
        observe_kernel,
        sds((8, NB, OB), F32),
        [SM, VM, VM, VM, VM],
        [pltpu.VMEM((256, NK * 128), BF16), pltpu.VMEM((NB, OB), F32)],
        3_000_000_000,
        2_000_000,
        24576,
        "observe",
    )(spans, key, spk, vb, columns)
    gathered = lax.all_to_all(copies, "mem", split_axis=0, concat_axis=0, tiled=True)
    lat, lon = call(
        halves_kernel,
        (sds((2, 256, 200), BF16), sds((2, 400, 400), BF16)),
        [HB, VM, VM],
        [pltpu.VMEM((256, 200), F32)],
        1_000_000,
        2_000_000,
        24576,
        "halves",
    )(copies, latitude_loc, longitude_loc)
    adjoint = call(
        adjoint_kernel,
        sds((16, 160, 128), F32),
        [SM, HB, VM, VM, VM, VM, VM],
        [pltpu.VMEM((128, NK * 128), F32), pltpu.VMEM((NB, OB), F32)],
        3_000_000_000,
        2_000_000,
        24576,
        "adjoint",
    )(spans, lat, key, spk, weight, vt, gathered)
    levels = lax.all_to_all(adjoint, "lev", split_axis=0, concat_axis=0, tiled=True)
    result = call(
        backward_kernel,
        sds((4, 200, 400), F32),
        [VM] * 4,
        [rows_scratch, pltpu.VMEM((800, 400), F32), pltpu.VMEM((4, 200, 400), F32), DMA((4,))],
        3_000_000_000,
        5_000_000,
        24576,
        "backward",
        HB,
    )(levels, c, lat, lon)
    return result[None]


def solution(mesh):
    placed = (
        P("mem", "lev", None, None),
        P("mem", None, None, None, "lev"),
        P("mem"),
        P(),
        P(),
        P(),
        P(None, "lev"),
        P(None, "lev"),
    )
    return jax.shard_map(
        body, mesh=mesh, in_specs=placed, out_specs=P("mem", "lev", None, None), check_vma=False
    )
```
